256 devices in a mesh: box: 16 (over z, y_hi), dir: 16 (over x, y_lo, core).
Axes of the slice: x: 4, y: 4 (y_hi: 2, y_lo: 2; y = y_hi * 2 + y_lo), z: 8, core: 2. Of those that a mesh axis runs over, the one named last changes fastest.
Arguments:
- pattern: bfloat16 [2, 64, 16, 128, 256], P(None, 'box', None, 'dir'), may hold values from -6 to 6
- occupied: int32 [64, 16], P('box'), may hold values from 0 to 1, as said below
- trans_fine: bfloat16 [2, 40, 128, 256], P(None, None, 'dir'), may hold values from -1.25 to 1.25
- trans_coarse: bfloat16 [2, 40, 256, 512], P(None, None, 'dir'), may hold values from -1.25 to 1.25
- theta_weights: bfloat16 [256, 4], P('dir'), may hold values from -0.19921875 to 0.796875
- phi_matrix: bfloat16 [256, 512], replicated, may hold values from -0.375 to 0.375
- child_phase: float32 [4, 256, 512], P(None, 'dir'), may hold values from -3.140625 to 3.140625
Outputs:
- local_fine: bfloat16 [2, 64, 16, 128, 256], P(None, 'box', None, 'dir')
- local_coarse: bfloat16 [2, 32, 8, 256, 512], P(None, 'box', None, 'dir')
The draws below stay inside these ranges and needn't reach their ends.
Inputs may be any that keep to these rules, and one draw needn't show every extreme that they name: `occupied`: 1 for a box that holds unknowns, 0 for an empty one.
All inputs are finite; a program needn't handle non-finite values.
Results may differ from the reference program's by a relative error of at most 0.0057.
Values may be sent and summed in bfloat16 or wider, within the bound.
A program may use at most 128 MiB of HBM per device.

```python
import jax
import jax.numpy as jnp
from jax import lax

RX = 4
NBY = 16
NTH1 = 128
NPH1 = 256
FAR = 40
NTH2 = 256
NPH2 = 512
NBX = 64


def draw_occupied(key, part):
    first_key = jax.random.fold_in(key, 11)
    second_key = jax.random.fold_in(key, 23)
    levels = jax.random.randint(first_key, (NBX // RX, 1, 1), 1, 5)
    levels = jnp.broadcast_to(levels, (NBX // RX, RX, NBY)).reshape(NBX, NBY)
    draws = jax.random.randint(second_key, (NBX, NBY), 0, 4)
    return (draws < levels).astype(jnp.int32)


def block_levels(stream_key, shape, shards, least, top_value):
    factor_of, own = 1.0, jax.random.fold_in(stream_key, 6)
    for dim, blocks in shards:
        steps = jnp.exp(jax.random.uniform(jax.random.fold_in(own, dim), (blocks,), jnp.float32, least / len(shards), top_value / len(shards)))
        factor_of = factor_of * jnp.repeat(steps, shape[dim] // blocks).reshape([-1 if axis == dim else 1 for axis in range(len(shape))])
    return factor_of


def normal_values(own_key, extent, deviation, limit, split=(), kind=jnp.bfloat16):
    level = block_levels(own_key, extent, split, -0.22, 0.18) if split else 1.0
    entries = jax.random.normal(own_key, extent, jnp.float32) * deviation * level
    return jnp.minimum(jnp.maximum(entries, -limit), limit).astype(kind)


def setup_inputs(seed: int = 0) -> dict:
    seeds = jax.random.split(jax.random.key(seed), 8)
    return {
        "pattern": normal_values(seeds[0], (2, NBX, NBY, NTH1, NPH1), 1.0, 6.0, ((1, 16), (3, 16))),
        "occupied": draw_occupied(jax.random.fold_in(seeds[7], 71), 0),
        "trans_fine": normal_values(seeds[2], (2, FAR, NTH1, NPH1), 27 ** -0.5, 1.25, ((2, 16),)),
        "trans_coarse": normal_values(seeds[3], (2, FAR, NTH2, NPH2), 27 ** -0.5, 1.25, ((2, 16),)),
        "theta_weights": jnp.clip(-0.19921875 + 0.99609375 * jax.random.uniform(seeds[4], (NTH2, 4), jnp.float32) ** block_levels(seeds[4], (NTH2, 4), ((0, 16),), -0.2, 0.2), -0.19921875, 0.796875).astype(jnp.bfloat16),
        "phi_matrix": normal_values(seeds[5], (NPH1, NPH2), NPH1 ** -0.5, 0.375),
        "child_phase": jnp.clip(jax.random.uniform(seeds[6], (4, NTH2, NPH2), jnp.float32, -3.140625, 3.140625), -3.140625, 3.140625),
    }


far_offsets = [(step_row, step_col) for step_row in range(-3, 4) for step_col in range(-3, 4) if max(abs(step_row), abs(step_col)) >= 2]


def allowed(parity, step):
    if step == 3:
        return 1.0 - parity
    if step == -3:
        return parity
    return jnp.ones_like(parity)


def translate(extended, table, occupied_dest, first_row):
    count_rows = extended.shape[1] - 6
    count_cols = extended.shape[2]
    padded = jnp.pad(extended, ((0, 0), (0, 0), (3, 3), (0, 0), (0, 0)))
    row_parity = ((first_row + jnp.arange(count_rows, dtype=jnp.int32)) % 2).astype(jnp.float32)
    col_parity = (jnp.arange(count_cols, dtype=jnp.int32) % 2).astype(jnp.float32)
    shape = (count_rows, count_cols, extended.shape[3], extended.shape[4])
    real_sum = jnp.zeros(shape, jnp.float32)
    imag_sum = jnp.zeros(shape, jnp.float32)
    for offset_code, (step_row, step_col) in enumerate(far_offsets):
        weight = allowed(row_parity, step_row)[:, None] * allowed(col_parity, step_col)[None, :]
        weight = weight[:, :, None, None]
        source = padded[:, 3 + step_row:3 + step_row + count_rows, 3 + step_col:3 + step_col + count_cols].astype(jnp.float32)
        factor_real = table[0, offset_code].astype(jnp.float32)
        factor_imag = table[1, offset_code].astype(jnp.float32)
        real_sum = real_sum + weight * (source[0] * factor_real - source[1] * factor_imag)
        imag_sum = imag_sum + weight * (source[0] * factor_imag + source[1] * factor_real)
    dest = occupied_dest.astype(jnp.float32)[:, :, None, None]
    return jnp.stack([real_sum * dest, imag_sum * dest])


def blocked_translate(source, table, occupied_dest, block):
    padded_rows = jnp.pad(source, ((0, 0), (3, 3), (0, 0), (0, 0), (0, 0)))
    count = source.shape[1] // block

    def one_block(index):
        start = (index * block).astype(jnp.int32)
        slab = lax.dynamic_slice_in_dim(padded_rows, start, block + 6, 1)
        dest = lax.dynamic_slice_in_dim(occupied_dest, start, block, 0)
        return translate(slab, table, dest, start).astype(jnp.bfloat16)

    result = lax.map(one_block, jnp.arange(count, dtype=jnp.int32))
    result = jnp.moveaxis(result, 0, 1)
    return result.reshape(2, count * block, source.shape[2], source.shape[3], source.shape[4])


def band_matrix(weights, columns):
    rows_count = weights.shape[0]
    row_ids = jnp.arange(rows_count, dtype=jnp.int32)[:, None]
    col_ids = jnp.arange(columns, dtype=jnp.int32)[None, :]
    band = jnp.zeros((rows_count, columns), jnp.float32)
    for stencil in range(4):
        band = band + jnp.where(col_ids == row_ids // 2 + 1 + stencil, weights[:, stencil:stencil + 1].astype(jnp.float32), 0.0)
    return band


def aggregate_block(slab, band, phi_matrix, phase_cos, phase_sin):
    theta_part = jnp.einsum('rc,xijcp->xijrp', band, slab.astype(jnp.float32)).astype(jnp.bfloat16)
    count_rows, count_cols = slab.shape[1], slab.shape[2]
    theta_rows, azimuths = band.shape[0], phi_matrix.shape[1]
    full = jnp.dot(theta_part.reshape(-1, phi_matrix.shape[0]), phi_matrix, preferred_element_type=jnp.float32)
    full = full.reshape(2, count_rows // 2, 2, count_cols // 2, 2, theta_rows, azimuths)
    real_part = jnp.sum(phase_cos * full[0] - phase_sin * full[1], axis=(1, 3))
    imag_part = jnp.sum(phase_cos * full[1] + phase_sin * full[0], axis=(1, 3))
    return jnp.stack([real_part, imag_part]).astype(jnp.bfloat16)


def reference(pattern, occupied, trans_fine, trans_coarse, theta_weights, phi_matrix, child_phase):
    masked = pattern * occupied.astype(jnp.bfloat16)[None, :, :, None, None]
    local_fine = blocked_translate(masked, trans_fine, occupied, RX)
    theta_padded = jnp.pad(masked, ((0, 0), (0, 0), (0, 0), (2, 2), (0, 0)))
    band = band_matrix(theta_weights, theta_padded.shape[3])
    phase_cos = jnp.cos(child_phase).reshape(2, 2, NTH2, NPH2)[None, :, None, :, :, :]
    phase_sin = jnp.sin(child_phase).reshape(2, 2, NTH2, NPH2)[None, :, None, :, :, :]
    count = NBX // RX

    def one_block(index):
        start = (index * RX).astype(jnp.int32)
        slab = lax.dynamic_slice_in_dim(theta_padded, start, RX, 1)
        return aggregate_block(slab, band, phi_matrix, phase_cos, phase_sin)

    coarse = lax.map(one_block, jnp.arange(count, dtype=jnp.int32))
    coarse = jnp.moveaxis(coarse, 0, 1).reshape(2, NBX // 2, NBY // 2, NTH2, NPH2)
    occupied_coarse = jnp.max(occupied.reshape(NBX // 2, 2, NBY // 2, 2), axis=(1, 3))
    local_coarse = blocked_translate(coarse, trans_coarse, occupied_coarse, RX // 2)
    return local_fine, local_coarse
```

```python
import functools

import jax
import jax.numpy as jnp
from jax import lax
from jax.experimental import pallas as pl
from jax.experimental.pallas import tpu as pltpu
from jax.sharding import PartitionSpec as P

MESH = pl.DeviceIdType.MESH
F32, BF16 = jnp.float32, jnp.bfloat16
VMEM = pl.BlockSpec(memory_space=pltpu.VMEM)
SMEM = pl.BlockSpec(memory_space=pltpu.SMEM)
ANY = pl.BlockSpec(memory_space=pl.ANY)

CODES = {
    pq: code
    for code, pq in enumerate(
        (p, q) for p in range(-3, 4) for q in range(-3, 4) if max(abs(p), abs(q)) >= 2
    )
}


def exchange_kernel(nb, nd, pat, occ, nbr, thb, tha, occn, ss, rs):
    b, d = lax.axis_index("box"), lax.axis_index("dir")
    yh = lax.rem(b, 2)
    cross = {"box": b + 1 - 2 * yh}
    ahead = {"box": lax.rem(b + 2 - 4 * yh + nb, nb)}
    behind = {"box": lax.rem(b - 2 + 4 * yh + nb, nb)}
    up, down = {"dir": lax.rem(d + 1, nd)}, {"dir": lax.rem(d + nd - 1, nd)}
    bar = pltpu.get_barrier_semaphore()
    for p in (cross, ahead, behind, up, down):
        pl.semaphore_signal(bar, inc=1, device_id=p, device_id_type=MESH)
    pl.semaphore_wait(bar, 5)
    rows, nt = pat.shape[1], pat.shape[3]
    count = iter(range(64))

    def send(src, dst, device):
        i = next(count)
        copy = pltpu.make_async_remote_copy(
            src_ref=src, dst_ref=dst, send_sem=ss.at[i], recv_sem=rs.at[i],
            device_id=device, device_id_type=MESH,
        )
        copy.start()
        return copy

    flags = send(occ, occn.at[0], cross)
    first = [send(pat.at[:, r], nbr.at[0, :, r], cross) for r in range(rows)]
    edges = [
        send(pat.at[:, :, :, nt - 2 : nt, :], thb.at[0], up),
        send(pat.at[:, :, :, 0:2, :], tha.at[0], down),
    ]
    flags.wait_recv()
    rest = [send(occn.at[0], occn.at[1], ahead)]
    middle = []
    for r in range(rows):
        first[r].wait_recv()
        rest.append(send(nbr.at[0, :, r], nbr.at[1, :, r], ahead))
        middle.append(
            (
                send(nbr.at[0, :, r, :, nt - 2 : nt, :], thb.at[1, :, r], up),
                send(nbr.at[0, :, r, :, 0:2, :], tha.at[1, :, r], down),
            )
        )
    for r in range(rows):
        before, after = middle[r]
        before.wait_recv()
        rest.append(send(thb.at[1, :, r], thb.at[2, :, r], ahead))
        after.wait_recv()
        rest.append(send(tha.at[1, :, r], tha.at[2, :, r], ahead))
    for copy in edges + rest:
        copy.wait()
    for copy in [flags] + first + [c for pair in middle for c in pair]:
        copy.wait_send()


def exchange(pattern, occupied, nb, nd):
    _, rows, cols, nt, nph = pattern.shape
    shape = jax.ShapeDtypeStruct
    return pl.pallas_call(
        functools.partial(exchange_kernel, nb, nd),
        out_shape=(
            shape((2, 2, rows, cols, nt, nph), BF16),
            shape((3, 2, rows, cols, 2, nph), BF16),
            shape((3, 2, rows, cols, 2, nph), BF16),
            shape((2, rows, cols), jnp.int32),
        ),
        in_specs=[ANY, ANY],
        out_specs=(ANY,) * 4,
        scratch_shapes=[pltpu.SemaphoreType.DMA((32,)), pltpu.SemaphoreType.DMA((32,))],
        compiler_params=pltpu.CompilerParams(collective_id=0, has_side_effects=True),
        name="exchange",
    )(pattern, occupied)


def m2l_parent(load, table, ncols, parent):
    acc = {}
    for s in range(6):
        for u in range(6):
            col = 2 * parent + u - 2
            if not 0 <= col < ncols:
                continue
            pairs = [
                (a, b, CODES[(s - 2 - a, u - 2 - b)])
                for a in range(2)
                for b in range(2)
                if (s - 2 - a, u - 2 - b) in CODES
            ]
            if not pairs:
                continue
            sre, sim = load(s, col)
            for a, b, code in pairs:
                tre, tim = table(code)
                re = sre * tre - sim * tim
                im = sre * tim + sim * tre
                if (a, b) in acc:
                    re, im = acc[(a, b)][0] + re, acc[(a, b)][1] + im
                acc[(a, b)] = (re, im)
    return acc


def lanes(i):
    return pl.ds(pl.multiple_of(i * 128, 128), 128)


def main_kernel(
    nb, nd, pat, nbr, thb, tha, occ, occn, trf, trc, wts, phi, cosr, sinr,
    outf, outc, xs, tf, tc, wb, tp, full, cs, phase,
):
    b, d = lax.axis_index("box"), lax.axis_index("dir")
    yh = lax.rem(b, 2)
    rows, cols, nt, nph = pat.shape[1:]
    nt2, nph2 = trc.shape[2:]
    has_above = (b > 0).astype(F32)
    has_below = (b < nb - 1).astype(F32)
    has_up = (d < nd - 1).astype(F32)
    has_down = (d > 0).astype(F32)

    def fill(read, read_before, read_after, flag, first_row, scale):
        def one(i, _):
            r, c = i // cols, lax.rem(i, cols)
            m = flag(r, c).astype(F32) * scale
            for k in range(2):
                xs[first_row + r, c, k, 8 : 8 + nt, :] = read(k, r, c).astype(F32) * m
                xs[first_row + r, c, k, 6:8, :] = read_before(k, r, c).astype(F32) * (m * has_down)
                xs[first_row + r, c, k, 8 + nt : 10 + nt, :] = read_after(k, r, c).astype(F32) * (m * has_up)
            return 0

        lax.fori_loop(0, rows * cols, one, 0)

    fill(
        lambda k, r, c: pat[k, r, c], lambda k, r, c: thb[0, k, r, c], lambda k, r, c: tha[0, k, r, c],
        lambda r, c: occ[r, c], rows, jnp.float32(1.0),
    )
    for slot, first_row, scale in ((1 - yh, 0, has_above), (yh, 2 * rows, has_below)):
        fill(
            lambda k, r, c, slot=slot: nbr[slot, k, r, c],
            lambda k, r, c, slot=slot: thb[1 + slot, k, r, c],
            lambda k, r, c, slot=slot: tha[1 + slot, k, r, c],
            lambda r, c, slot=slot: occn[slot, r, c], first_row, scale,
        )

    far = trf.shape[1]

    def widen(i, _):
        for k in range(2):
            tf[k, i] = trf[k, i].astype(F32)
            tc[k, i] = trc[k, i].astype(F32)
        return 0

    lax.fori_loop(0, far, widen, 0)
    w = wts[...].astype(F32)
    for m in range(4):
        wb[m] = jnp.broadcast_to(w[:, m : m + 1], (nt2, 128))
    for q in range(nph2 // 128):
        for ab in range(4):
            phase[0, ab, q] = cosr[ab, :, 128 * q : 128 * q + 128]
            phase[1, ab, q] = sinr[ab, :, 128 * q : 128 * q + 128]

    half = cols // 2

    def aggregate(i, _):
        row, part = i // 2, lax.rem(i, 2)
        weights = [[wb[m, pl.ds(e, nt, stride=2), :] for m in range(4)] for e in range(2)]
        for a in range(2):
            for c in range(half):
                for k in range(2):
                    x = [xs[2 * row + a, part * half + c, k, 7 + m : 7 + m + nt, :] for m in range(4)]
                    eo = []
                    for e in range(2):
                        pieces = []
                        for q in range(nph // 128):
                            s = slice(128 * q, 128 * q + 128)
                            t01 = weights[e][0] * x[0][:, s] + weights[e][1] * x[1][:, s]
                            t23 = weights[e][2] * x[2][:, s] + weights[e][3] * x[3][:, s]
                            pieces.append(t01 + t23)
                        eo.append(jnp.concatenate(pieces, axis=1))
                    at = ((a * half + c) * 2 + k) * nt2
                    tp[at : at + nt2, :] = jnp.concatenate(eo, axis=0).astype(BF16)
        full[...] = jnp.dot(tp[...], phi[...], preferred_element_type=F32)
        for e in range(2):
            for q in range(nph2 // 128):
                s = slice(128 * q, 128 * q + 128)
                ph = [
                    (phase[0, ab, q, pl.ds(e, nt, stride=2), :], phase[1, ab, q, pl.ds(e, nt, stride=2), :])
                    for ab in range(4)
                ]
                for parent in range(half // 2):
                    re = im = None
                    for a in range(2):
                        for bb in range(2):
                            at = (a * half + 2 * parent + bb) * 2 * nt2 + e * nt
                            fre = full[at : at + nt, s]
                            fim = full[at + nt2 : at + nt2 + nt, s]
                            co, si = ph[2 * a + bb]
                            tre, tim = co * fre - si * fim, co * fim + si * fre
                            re, im = (tre, tim) if re is None else (re + tre, im + tim)
                    cs[row, part * (half // 2) + parent, 0, q, pl.ds(e, nt, stride=2), :] = re
                    cs[row, part * (half // 2) + parent, 1, q, pl.ds(e, nt, stride=2), :] = im
        return 0

    lax.fori_loop(0, 3 * rows, aggregate, 0)

    def fine(i, _):
        block, q = i // (nph // 128), lanes(lax.rem(i, nph // 128))
        for parent in range(cols // 2):
            acc = m2l_parent(
                lambda s, col: tuple(xs[rows - 2 + 2 * block + s, col, k, 8 : 8 + nt, q] for k in range(2)),
                lambda code: (tf[0, code, :, q], tf[1, code, :, q]),
                cols, parent,
            )
            for (a, bb), value in acc.items():
                r, c = 2 * block + a, 2 * parent + bb
                m = occ[r, c].astype(F32)
                for k in range(2):
                    outf[k, r, c, :, q] = (value[k] * m).astype(BF16)
        return 0

    lax.fori_loop(0, (rows // 2) * (nph // 128), fine, 0)

    coarse_rows, coarse_cols = rows // 2, cols // 2

    def coarse(i, _):
        t = pl.ds(pl.multiple_of(lax.rem(i, nt2 // 8) * 8, 8), 8)
        tile = i // (nt2 // 8)
        q = lanes(tile)
        for parent in range(coarse_cols // 2):
            acc = m2l_parent(
                lambda s, col: (cs[s, col, 0, tile, t, :], cs[s, col, 1, tile, t, :]),
                lambda code: (tc[0, code, t, q], tc[1, code, t, q]),
                coarse_cols, parent,
            )
            for (a, bb), value in acc.items():
                c = 2 * parent + bb
                m = jnp.maximum(
                    jnp.maximum(occ[2 * a, 2 * c], occ[2 * a, 2 * c + 1]),
                    jnp.maximum(occ[2 * a + 1, 2 * c], occ[2 * a + 1, 2 * c + 1]),
                ).astype(F32)
                for k in range(2):
                    outc[k, a, c, t, q] = (value[k] * m).astype(BF16)
        return 0

    lax.fori_loop(0, (nt2 // 8) * (nph2 // 128), coarse, 0)


def local(nb, nd, pattern, occupied, trans_fine, trans_coarse, theta_weights, phi_matrix, child_phase):
    _, rows, cols, nt, nph = pattern.shape
    far, nt2, nph2 = trans_coarse.shape[1:]
    nbr, thb, tha, occn = exchange(pattern, occupied, nb, nd)
    shape = jax.ShapeDtypeStruct
    return pl.pallas_call(
        functools.partial(main_kernel, nb, nd),
        out_shape=(
            shape((2, rows, cols, nt, nph), BF16),
            shape((2, rows // 2, cols // 2, nt2, nph2), BF16),
        ),
        in_specs=[VMEM] * 4 + [SMEM] * 2 + [VMEM] * 6,
        out_specs=(VMEM, VMEM),
        scratch_shapes=[
            pltpu.VMEM((3 * rows, cols, 2, nt + 16, nph), F32),
            pltpu.VMEM((2, far, nt, nph), F32),
            pltpu.VMEM((2, far, nt2, nph2), F32),
            pltpu.VMEM((4, nt2, 128), F32),
            pltpu.VMEM((2 * (cols // 2) * 2 * nt2, nph), BF16),
            pltpu.VMEM((2 * (cols // 2) * 2 * nt2, nph2), F32),
            pltpu.VMEM((3 * rows // 2, cols // 2, 2, nph2 // 128, nt2, 128), F32),
            pltpu.VMEM((2, 4, nph2 // 128, nt2, 128), F32),
        ],
        compiler_params=pltpu.CompilerParams(vmem_limit_bytes=60 * 1024 * 1024),
        name="main",
    )(
        pattern, nbr, thb, tha, occupied, occn, trans_fine, trans_coarse, theta_weights, phi_matrix,
        jnp.cos(child_phase), jnp.sin(child_phase),
    )


def solution(mesh):
    return jax.shard_map(
        functools.partial(local, mesh.shape["box"], mesh.shape["dir"]),
        mesh=mesh,
        in_specs=(
            P(None, "box", None, "dir", None),
            P("box", None),
            P(None, None, "dir", None),
            P(None, None, "dir", None),
            P("dir", None),
            P(),
            P(None, "dir", None),
        ),
        out_specs=(P(None, "box", None, "dir", None), P(None, "box", None, "dir", None)),
        check_vma=False,
    )
```

```python
import functools

import jax
import jax.numpy as jnp
from jax import lax
from jax.experimental import pallas as pl
from jax.experimental.pallas import tpu as pltpu
from jax.sharding import PartitionSpec as P

MESH = pl.DeviceIdType.MESH
F32, BF16 = jnp.float32, jnp.bfloat16
VMEM = pl.BlockSpec(memory_space=pltpu.VMEM)
SMEM = pl.BlockSpec(memory_space=pltpu.SMEM)
ANY = pl.BlockSpec(memory_space=pl.ANY)

CODES = {
    pq: code
    for code, pq in enumerate(
        (p, q) for p in range(-3, 4) for q in range(-3, 4) if max(abs(p), abs(q)) >= 2
    )
}


def loop(start, stop, body):
    def step(i, carry):
        body(i)
        return carry

    lax.fori_loop(start, stop, step, 0)


def lanes(i):
    return pl.ds(pl.multiple_of(i * 128, 128), 128)


def m2l_pass(sources, load, table, first, store, ncols):
    def parent_sums(parent, window):
        acc = {}
        if first is not None:
            for a in range(2):
                for b in range(2):
                    acc[(a, b)] = tuple(first(k, a, 2 * parent + b) for k in range(2))
        for s in sources:
            for u in window:
                pairs = [
                    (a, b, CODES[(s - 2 - a, u - 2 - b)])
                    for a in range(2)
                    for b in range(2)
                    if (s - 2 - a, u - 2 - b) in CODES
                ]
                if not pairs:
                    continue
                sre, sim = load(s, 2 * parent + u - 2)
                for a, b, code in pairs:
                    tre, tim = table(code)
                    re = sre * tre - sim * tim
                    im = sre * tim + sim * tre
                    if (a, b) in acc:
                        re, im = acc[(a, b)][0] + re, acc[(a, b)][1] + im
                    acc[(a, b)] = (re, im)
        for (a, b), value in acc.items():
            for k in range(2):
                store(k, a, 2 * parent + b, value[k])

    parent_sums(0, range(2, 6))
    loop(1, ncols // 2 - 1, lambda parent: parent_sums(parent, range(6)))
    parent_sums(ncols // 2 - 1, range(4))


def kernel(
    nb, nd, pat, occ_any, occ, trf_any, trc_any, wts, phi_any, child_any,
    outf, outc,
    patv, nbr, thb, tha, flagv, flags, trf, trc, phi, child,
    xs, tf, tc, wb, tp, full, cs, phase, accf, accc,
    ss, rs, ls,
):
    b, d = lax.axis_index("box"), lax.axis_index("dir")
    yh = lax.rem(b, 2)
    cross = {"box": b + 1 - 2 * yh}
    ahead = {"box": lax.rem(b + 2 - 4 * yh + nb, nb)}
    behind = {"box": lax.rem(b - 2 + 4 * yh + nb, nb)}
    up, down = {"dir": lax.rem(d + 1, nd)}, {"dir": lax.rem(d + nd - 1, nd)}
    rows, cols, nt, nph = patv.shape[1:]
    nt2, nph2 = trc.shape[2:]
    far = trf.shape[1]
    half = cols // 2
    tiles, tiles2 = nph // 128, nph2 // 128

    bar = pltpu.get_barrier_semaphore()
    for p in (cross, ahead, behind, up, down):
        pl.semaphore_signal(bar, inc=1, device_id=p, device_id_type=MESH)
    local = [
        pltpu.make_async_copy(src, dst, ls.at[i])
        for i, (src, dst) in enumerate(
            ((pat, patv), (trf_any, trf), (trc_any, trc), (child_any, child), (phi_any, phi))
        )
    ]
    for copy in local:
        copy.start()

    count = iter(range(64))

    def send(src, dst, device):
        i = next(count)
        copy = pltpu.make_async_remote_copy(
            src_ref=src, dst_ref=dst, send_sem=ss.at[i], recv_sem=rs.at[i],
            device_id=device, device_id_type=MESH,
        )
        copy.start()
        return copy

    has_up = (d < nd - 1).astype(F32)
    has_down = (d > 0).astype(F32)
    other = b - 1 + 2 * yh
    has_other = ((other >= 0).astype(jnp.int32) * (other < nb).astype(jnp.int32)).astype(F32)

    def fill(read, flag, first_row):
        def row(r):
            for c in range(cols):
                m = flag(r, c)
                for k in range(2):
                    xs[first_row + r, c, k, 8 : 8 + nt, :] = read(k, r, c).astype(F32) * m

        loop(0, rows, row)

    def fill_edges(slot, flag, first_row):
        def row(r):
            for c in range(cols):
                m = flag(r, c)
                for k in range(2):
                    xs[first_row + r, c, k, 6:8, :] = thb[slot, k, r, c].astype(F32) * (m * has_down)
                    xs[first_row + r, c, k, 8 + nt : 10 + nt, :] = tha[slot, k, r, c].astype(F32) * (m * has_up)

        loop(0, rows, row)

    def own_flag(r, c):
        return occ[r, c].astype(F32)

    def cross_flag(r, c):
        return flags[0, r, c].astype(F32)

    def other_flag(r, c):
        return flags[1, r, c].astype(F32) * has_other

    local[0].wait()
    fill(lambda k, r, c: patv[k, r, c], own_flag, rows)

    pl.semaphore_wait(bar, 5)
    flag_copy = send(occ_any, flagv.at[0], cross)
    first = [send(pat.at[:, r], nbr.at[0, :, r], cross) for r in range(rows)]
    own_edges = [
        send(pat.at[:, :, :, nt - 2 : nt, :], thb.at[0], up),
        send(pat.at[:, :, :, 0:2, :], tha.at[0], down),
    ]
    onward, cross_edges, other_edges = [], [], []

    def hand_on(r):
        first[r].wait_recv()
        onward.append(send(nbr.at[0, :, r], nbr.at[1, :, r], ahead))
        cross_edges.append(send(nbr.at[0, :, r, :, nt - 2 : nt, :], thb.at[1, :, r], up))
        cross_edges.append(send(nbr.at[0, :, r, :, 0:2, :], tha.at[1, :, r], down))

    def pass_edges(r):
        onward[r].wait_recv()
        other_edges.append(send(nbr.at[1, :, r, :, nt - 2 : nt, :], thb.at[2, :, r], up))
        other_edges.append(send(nbr.at[1, :, r, :, 0:2, :], tha.at[2, :, r], down))

    local[1].wait()
    local[2].wait()

    def widen(i):
        for k in range(2):
            tf[k, i] = trf[k, i].astype(F32)
            tc[k, i] = trc[k, i].astype(F32)

    loop(0, far, widen)
    eye = (
        lax.broadcasted_iota(jnp.int32, (nt2, nt2), 0) == lax.broadcasted_iota(jnp.int32, (nt2, nt2), 1)
    ).astype(F32)
    w = wts[...].astype(F32)
    for m in range(4):
        column = jnp.sum(eye * w[m : m + 1, :], axis=1, keepdims=True)
        wb[m] = jnp.broadcast_to(column, (nt2, 128))
    local[3].wait()

    def phases(ab):
        for q in range(tiles2):
            angle = child[ab, :, 128 * q : 128 * q + 128]
            phase[0, ab, q] = jnp.cos(angle)
            phase[1, ab, q] = jnp.sin(angle)

    loop(0, 4, phases)

    flag_copy.wait_recv()
    flag_on = send(flagv.at[0], flagv.at[1], ahead)
    hand_on(0)

    def fine(block, sources, start, final):
        def tile(q):
            s128 = lanes(q)

            def store(k, a, c, value):
                r = 2 * block + a
                if not final:
                    accf[k, r, c, :, s128] = value
                else:
                    outf[k, r, c, :, s128] = (value * occ[r, c].astype(F32)).astype(BF16)

            m2l_pass(
                sources,
                lambda s, c: tuple(xs[rows - 2 + 2 * block + s, c, k, 8 : 8 + nt, s128] for k in range(2)),
                lambda code: (tf[0, code, :, s128], tf[1, code, :, s128]),
                None if start else (lambda k, a, c: accf[k, 2 * block + a, c, :, s128]),
                store, cols,
            )

        loop(0, tiles, tile)

    def aggregate(first_row):
        def part_of(i):
            row, part = first_row + i // 2, lax.rem(i, 2)
            weights = [[wb[m, pl.ds(e, nt, stride=2), :] for m in range(4)] for e in range(2)]
            for a in range(2):
                for c in range(half):
                    for k in range(2):
                        x = [xs[2 * row + a, part * half + c, k, 7 + m : 7 + m + nt, :] for m in range(4)]
                        eo = []
                        for e in range(2):
                            pieces = []
                            for q in range(tiles):
                                s = slice(128 * q, 128 * q + 128)
                                t01 = weights[e][0] * x[0][:, s] + weights[e][1] * x[1][:, s]
                                t23 = weights[e][2] * x[2][:, s] + weights[e][3] * x[3][:, s]
                                pieces.append(t01 + t23)
                            eo.append(jnp.concatenate(pieces, axis=1))
                        at = ((a * half + c) * 2 + k) * nt2
                        tp[at : at + nt2, :] = jnp.concatenate(eo, axis=0).astype(BF16)
            full[...] = jnp.dot(tp[...], phi[...], preferred_element_type=F32)
            for e in range(2):
                for q in range(tiles2):
                    s = slice(128 * q, 128 * q + 128)
                    ph = [
                        (phase[0, ab, q, pl.ds(e, nt, stride=2), :], phase[1, ab, q, pl.ds(e, nt, stride=2), :])
                        for ab in range(4)
                    ]
                    for parent in range(half // 2):
                        re = im = None
                        for a in range(2):
                            for bb in range(2):
                                at = (a * half + 2 * parent + bb) * 2 * nt2 + e * nt
                                fre = full[at : at + nt, s]
                                fim = full[at + nt2 : at + nt2 + nt, s]
                                co, si = ph[2 * a + bb]
                                tre, tim = co * fre - si * fim, co * fim + si * fre
                                re, im = (tre, tim) if re is None else (re + tre, im + tim)
                        cs[row, part * (half // 2) + parent, 0, q, pl.ds(e, nt, stride=2), :] = re
                        cs[row, part * (half // 2) + parent, 1, q, pl.ds(e, nt, stride=2), :] = im

        loop(0, rows, part_of)

    def coarse(sources, start, final):
        def tile(i):
            t = pl.ds(pl.multiple_of(lax.rem(i, nt2 // 8) * 8, 8), 8)
            q = i // (nt2 // 8)
            s128 = lanes(q)

            def store(k, a, c, value):
                if not final:
                    accc[k, a, c, q, t, :] = value
                else:
                    m = jnp.maximum(
                        jnp.maximum(occ[2 * a, 2 * c], occ[2 * a, 2 * c + 1]),
                        jnp.maximum(occ[2 * a + 1, 2 * c], occ[2 * a + 1, 2 * c + 1]),
                    ).astype(F32)
                    outc[k, a, c, t, s128] = (value * m).astype(BF16)

            m2l_pass(
                sources,
                lambda s, c: (cs[s, c, 0, q, t, :], cs[s, c, 1, q, t, :]),
                lambda code: (tc[0, code, t, s128], tc[1, code, t, s128]),
                None if start else (lambda k, a, c: accc[k, a, c, q, t, :]),
                store, half,
            )

        loop(0, (nt2 // 8) * tiles2, tile)

    last = rows // 2 - 1
    fine(0, range(2, 6), True, False)
    hand_on(1)
    fine(1, range(0, 4), True, False)
    hand_on(2)
    for copy in own_edges:
        copy.wait_recv()
    fill_edges(0, own_flag, rows)
    local[4].wait()
    aggregate(rows // 2)
    hand_on(3)
    coarse(range(2, 4), True, False)

    to_flags = pltpu.make_async_copy(flagv.at[0], flags.at[0], ls.at[5])
    to_flags.start()
    to_flags.wait()
    fill(lambda k, r, c: nbr[0, k, r, c], cross_flag, 2 * rows * (1 - yh))
    pass_edges(0)

    @pl.when(yh == 0)
    def _():
        fine(last, range(4, 6), False, True)

    @pl.when(yh == 1)
    def _():
        fine(0, range(0, 2), False, True)

    pass_edges(1)
    for copy in cross_edges:
        copy.wait_recv()
    fill_edges(1, cross_flag, 2 * rows * (1 - yh))
    aggregate(rows * (1 - yh))
    pass_edges(2)

    @pl.when(yh == 0)
    def _():
        coarse(range(4, 6), False, False)

    @pl.when(yh == 1)
    def _():
        coarse(range(0, 2), False, False)

    flag_on.wait_recv()
    to_flags = pltpu.make_async_copy(flagv.at[1], flags.at[1], ls.at[5])
    to_flags.start()
    to_flags.wait()
    pass_edges(3)
    fill(lambda k, r, c: nbr[1, k, r, c], other_flag, 2 * rows * yh)

    @pl.when(yh == 0)
    def _():
        fine(0, range(0, 2), False, True)

    @pl.when(yh == 1)
    def _():
        fine(last, range(4, 6), False, True)

    for copy in other_edges:
        copy.wait_recv()
    fill_edges(2, other_flag, 2 * rows * yh)
    aggregate(rows * yh)

    @pl.when(yh == 0)
    def _():
        coarse(range(0, 2), False, True)

    @pl.when(yh == 1)
    def _():
        coarse(range(4, 6), False, True)

    for copy in [flag_copy, flag_on] + first + own_edges + onward + cross_edges + other_edges:
        copy.wait_send()


def local_step(nb, nd, pattern, occupied, trans_fine, trans_coarse, theta_weights, phi_matrix, child_phase):
    _, rows, cols, nt, nph = pattern.shape
    far, nt2, nph2 = trans_coarse.shape[1:]
    shape = jax.ShapeDtypeStruct
    tile2 = nph2 // 128
    return pl.pallas_call(
        functools.partial(kernel, nb, nd),
        out_shape=(
            shape((2, rows, cols, nt, nph), BF16),
            shape((2, rows // 2, cols // 2, nt2, nph2), BF16),
        ),
        in_specs=[ANY, ANY, SMEM, ANY, ANY, VMEM, ANY, ANY],
        out_specs=(VMEM, VMEM),
        scratch_shapes=[
            pltpu.VMEM((2, rows, cols, nt, nph), BF16),
            pltpu.VMEM((2, 2, rows, cols, nt, nph), BF16),
            pltpu.VMEM((3, 2, rows, cols, 2, nph), BF16),
            pltpu.VMEM((3, 2, rows, cols, 2, nph), BF16),
            pltpu.VMEM((2, rows, cols), jnp.int32),
            pltpu.SMEM((2, rows, cols), jnp.int32),
            pltpu.VMEM((2, far, nt, nph), BF16),
            pltpu.VMEM((2, far, nt2, nph2), BF16),
            pltpu.VMEM(phi_matrix.shape, BF16),
            pltpu.VMEM((4, nt2, nph2), F32),
            pltpu.VMEM((3 * rows, cols, 2, nt + 16, nph), F32),
            pltpu.VMEM((2, far, nt, nph), F32),
            pltpu.VMEM((2, far, nt2, nph2), F32),
            pltpu.VMEM((4, nt2, 128), F32),
            pltpu.VMEM((2 * (cols // 2) * 2 * nt2, nph), BF16),
            pltpu.VMEM((2 * (cols // 2) * 2 * nt2, nph2), F32),
            pltpu.VMEM((3 * rows // 2, cols // 2, 2, tile2, nt2, 128), F32),
            pltpu.VMEM((2, 4, tile2, nt2, 128), F32),
            pltpu.VMEM((2, rows, cols, nt, nph), F32),
            pltpu.VMEM((2, rows // 2, cols // 2, tile2, nt2, 128), F32),
            pltpu.SemaphoreType.DMA((32,)),
            pltpu.SemaphoreType.DMA((32,)),
            pltpu.SemaphoreType.DMA((6,)),
        ],
        compiler_params=pltpu.CompilerParams(
            collective_id=0, has_side_effects=True, vmem_limit_bytes=60 * 1024 * 1024
        ),
        name="main",
    )(pattern, occupied, occupied, trans_fine, trans_coarse, theta_weights.T, phi_matrix, child_phase)


def solution(mesh):
    return jax.shard_map(
        functools.partial(local_step, mesh.shape["box"], mesh.shape["dir"]),
        mesh=mesh,
        in_specs=(
            P(None, "box", None, "dir", None),
            P("box", None),
            P(None, None, "dir", None),
            P(None, None, "dir", None),
            P("dir", None),
            P(),
            P(None, "dir", None),
        ),
        out_specs=(P(None, "box", None, "dir", None), P(None, "box", None, "dir", None)),
        check_vma=False,
    )
```

```python
import functools

import jax
import jax.numpy as jnp
from jax import lax
from jax.experimental import pallas as pl
from jax.experimental.pallas import tpu as pltpu
from jax.sharding import PartitionSpec as P

MESH = pl.DeviceIdType.MESH
F32, BF16 = jnp.float32, jnp.bfloat16
VMEM = pl.BlockSpec(memory_space=pltpu.VMEM)
HBM = pl.BlockSpec(memory_space=pltpu.HBM)
ANY = pl.BlockSpec(memory_space=pl.ANY)

CODES = {
    pq: code
    for code, pq in enumerate(
        (p, q) for p in range(-3, 4) for q in range(-3, 4) if max(abs(p), abs(q)) >= 2
    )
}


def loop(start, stop, body):
    def step(i, carry):
        body(i)
        return carry

    lax.fori_loop(start, stop, step, 0)


def lanes(i):
    return pl.ds(pl.multiple_of(i * 128, 128), 128)


def m2l_pass(sources, load, table, first, store, ncols):
    def parent_sums(parent, window):
        acc = {}
        if first is not None:
            for a in range(2):
                for b in range(2):
                    acc[(a, b)] = tuple(first(k, a, 2 * parent + b) for k in range(2))
        for s in sources:
            for u in window:
                pairs = [
                    (a, b, CODES[(s - 2 - a, u - 2 - b)])
                    for a in range(2)
                    for b in range(2)
                    if (s - 2 - a, u - 2 - b) in CODES
                ]
                if not pairs:
                    continue
                sre, sim = load(s, 2 * parent + u - 2)
                for a, b, code in pairs:
                    tre, tim = table(code)
                    re = sre * tre - sim * tim
                    im = sre * tim + sim * tre
                    if (a, b) in acc:
                        re, im = acc[(a, b)][0] + re, acc[(a, b)][1] + im
                    acc[(a, b)] = (re, im)
        for (a, b), value in acc.items():
            for k in range(2):
                store(k, a, 2 * parent + b, value[k])

    parent_sums(0, range(2, 6))
    loop(1, ncols // 2 - 1, lambda parent: parent_sums(parent, range(6)))
    parent_sums(ncols // 2 - 1, range(4))


def kernel(
    nb, nd, pat, occ_any, trf_any, trc_any, wts_any, phi_any, child_any,
    outf, outc,
    patv, nbr, lasts, thb, tha, flagv, flags, occ, trf, trc, wts, phi, child,
    xs, tf, tc, wb, tp, full, cs, phase, accf, accc,
    ss, rs, ls,
):
    b, d = lax.axis_index("box"), lax.axis_index("dir")
    yh = lax.rem(b, 2)
    cross = {"box": b + 1 - 2 * yh}
    ahead = {"box": lax.rem(b + 2 - 4 * yh + nb, nb)}
    behind = {"box": lax.rem(b - 2 + 4 * yh + nb, nb)}
    up, down = {"dir": lax.rem(d + 1, nd)}, {"dir": lax.rem(d + nd - 1, nd)}
    rows, cols, nt, nph = patv.shape[1:]
    nt2, nph2 = trc.shape[2:]
    far = trf.shape[1]
    half = cols // 2
    tiles, tiles2 = nph // 128, nph2 // 128

    bar = pltpu.get_barrier_semaphore()
    for p in (cross, ahead, behind, up, down):
        pl.semaphore_signal(bar, inc=1, device_id=p, device_id_type=MESH)
    local = [
        pltpu.make_async_copy(src, dst, ls.at[i])
        for i, (src, dst) in enumerate(
            (
                (pat, patv), (occ_any, occ), (trf_any, trf), (trc_any, trc), (wts_any, wts),
                (child_any, child), (phi_any, phi),
            )
        )
    ]
    for copy in local:
        copy.start()

    count = iter(range(64))

    def send(src, dst, device):
        i = next(count)
        copy = pltpu.make_async_remote_copy(
            src_ref=src, dst_ref=dst, send_sem=ss.at[i], recv_sem=rs.at[i],
            device_id=device, device_id_type=MESH,
        )
        copy.start()
        return copy

    has_up = (d < nd - 1).astype(F32)
    has_down = (d > 0).astype(F32)
    other = b - 1 + 2 * yh
    has_other = ((other >= 0).astype(jnp.int32) * (other < nb).astype(jnp.int32)).astype(F32)

    def fill(slot, read, flag, first_row, r):
        for c in range(cols):
            m = flag(r, c)
            for k in range(2):
                xs[first_row + r, c, k, 8 : 8 + nt, :] = read(k, r, c).astype(F32) * m
        for c in range(cols):
            pair = [xs[first_row + r, c, k, 7 + nt : 8 + nt, :] for k in range(2)]
            lasts[slot, r, c] = jnp.concatenate(pair, axis=0).astype(BF16)

    def fill_edges(slot, flag, first_row, some):
        def row(r):
            for c in range(cols):
                m = flag(r, c) * has_up
                before = thb[slot, r, c].astype(F32) * has_down
                for k in range(2):
                    xs[first_row + r, c, k, 7:8, :] = before[k : k + 1]
                    xs[first_row + r, c, k, 8 + nt : 10 + nt, :] = tha[slot, k, r, c].astype(F32) * m

        loop(some[0], some[-1] + 1, row)

    def own_flag(r, c):
        return occ[r, c].astype(F32)

    def cross_flag(r, c):
        return flags[0, r, c].astype(F32)

    def other_flag(r, c):
        return flags[1, r, c].astype(F32) * has_other

    local[0].wait()
    local[1].wait()
    loop(0, rows, lambda r: fill(0, lambda k, r, c: patv[k, r, c], own_flag, rows, r))

    pl.semaphore_wait(bar, 5)
    first = [send(pat.at[:, 0], nbr.at[0, :, 0], cross)]
    flag_copy = send(occ_any, flagv.at[0], cross)
    own_edges = [
        send(lasts.at[0], thb.at[0], up),
        send(pat.at[:, :, :, 0:2, :], tha.at[0], down),
    ]
    first += [send(pat.at[:, r], nbr.at[0, :, r], cross) for r in range(1, rows)]
    onward, cross_edges, other_edges = [], [], []
    cross_row, other_row = 2 * rows * (1 - yh), 2 * rows * yh

    def hand_on(r):
        first[r].wait_recv()
        onward.append(send(nbr.at[0, :, r], nbr.at[1, :, r], ahead))
        cross_edges.append(send(nbr.at[0, :, r, :, 0:2, :], tha.at[1, :, r], down))
        fill(1, lambda k, r, c: nbr[0, k, r, c], cross_flag, cross_row, r)
        cross_edges.append(send(lasts.at[1, r], thb.at[1, r], up))

    def pass_edges(r):
        onward[r].wait_recv()
        other_edges.append(send(nbr.at[1, :, r, :, 0:2, :], tha.at[2, :, r], down))
        fill(2, lambda k, r, c: nbr[1, k, r, c], other_flag, other_row, r)
        other_edges.append(send(lasts.at[2, r], thb.at[2, r], up))

    def have(edges, slot, flag, first_row, some):
        for r in some:
            edges[2 * r].wait_recv()
            edges[2 * r + 1].wait_recv()
        fill_edges(slot, flag, first_row, some)

    local[2].wait()
    local[3].wait()

    def widen(i):
        for k in range(2):
            tf[k, i] = trf[k, i].astype(F32)
            tc[k, i] = trc[k, i].astype(F32)

    loop(0, far, widen)
    eye = (
        lax.broadcasted_iota(jnp.int32, (nt2, nt2), 0) == lax.broadcasted_iota(jnp.int32, (nt2, nt2), 1)
    ).astype(F32)
    local[4].wait()
    w = wts[...].astype(F32)
    for m in range(4):
        column = jnp.sum(eye * w[m : m + 1, :], axis=1, keepdims=True)
        wb[m] = jnp.broadcast_to(column, (nt2, 128))
    local[5].wait()

    def phases(ab):
        for q in range(tiles2):
            angle = child[ab, :, 128 * q : 128 * q + 128]
            phase[0, ab, q] = jnp.cos(angle)
            phase[1, ab, q] = jnp.sin(angle)

    loop(0, 4, phases)

    flag_copy.wait_recv()
    flag_on = send(flagv.at[0], flagv.at[1], ahead)
    to_flags = pltpu.make_async_copy(flagv.at[0], flags.at[0], ls.at[7])
    to_flags.start()
    to_flags.wait()
    hand_on(0)

    def fine(block, sources, start, final):
        def tile(q):
            s128 = lanes(q)

            def store(k, a, c, value):
                r = 2 * block + a
                if not final:
                    accf[k, r, c, :, s128] = value
                else:
                    outf[k, r, c, :, s128] = (value * occ[r, c].astype(F32)).astype(BF16)

            m2l_pass(
                sources,
                lambda s, c: tuple(xs[rows - 2 + 2 * block + s, c, k, 8 : 8 + nt, s128] for k in range(2)),
                lambda code: (tf[0, code, :, s128], tf[1, code, :, s128]),
                None if start else (lambda k, a, c: accf[k, 2 * block + a, c, :, s128]),
                store, cols,
            )

        loop(0, tiles, tile)

    def aggregate(row):
        def part_of(part):
            weights = [[wb[m, pl.ds(e, nt, stride=2), :] for m in range(4)] for e in range(2)]
            for a in range(2):
                for c in range(half):
                    for k in range(2):
                        x = [xs[2 * row + a, part * half + c, k, 7 + m : 7 + m + nt, :] for m in range(4)]
                        eo = []
                        for e in range(2):
                            pieces = []
                            for q in range(tiles):
                                s = slice(128 * q, 128 * q + 128)
                                t01 = weights[e][0] * x[0][:, s] + weights[e][1] * x[1][:, s]
                                t23 = weights[e][2] * x[2][:, s] + weights[e][3] * x[3][:, s]
                                pieces.append(t01 + t23)
                            eo.append(jnp.concatenate(pieces, axis=1))
                        at = ((a * half + c) * 2 + k) * nt2
                        tp[at : at + nt2, :] = jnp.concatenate(eo, axis=0).astype(BF16)
            full[...] = jnp.dot(tp[...], phi[...], preferred_element_type=F32)
            for e in range(2):
                for q in range(tiles2):
                    s = slice(128 * q, 128 * q + 128)
                    ph = [
                        (phase[0, ab, q, pl.ds(e, nt, stride=2), :], phase[1, ab, q, pl.ds(e, nt, stride=2), :])
                        for ab in range(4)
                    ]
                    for parent in range(half // 2):
                        re = im = None
                        for a in range(2):
                            for bb in range(2):
                                at = (a * half + 2 * parent + bb) * 2 * nt2 + e * nt
                                fre = full[at : at + nt, s]
                                fim = full[at + nt2 : at + nt2 + nt, s]
                                co, si = ph[2 * a + bb]
                                tre, tim = co * fre - si * fim, co * fim + si * fre
                                re, im = (tre, tim) if re is None else (re + tre, im + tim)
                        cs[row, part * (half // 2) + parent, 0, q, pl.ds(e, nt, stride=2), :] = re
                        cs[row, part * (half // 2) + parent, 1, q, pl.ds(e, nt, stride=2), :] = im

        loop(0, 2, part_of)

    def coarse(sources, start, final):
        def tile(i):
            t = pl.ds(pl.multiple_of(lax.rem(i, nt2 // 8) * 8, 8), 8)
            q = i // (nt2 // 8)
            s128 = lanes(q)

            def store(k, a, c, value):
                if not final:
                    accc[k, a, c, q, t, :] = value
                else:
                    m = jnp.maximum(
                        jnp.maximum(occ[2 * a, 2 * c], occ[2 * a, 2 * c + 1]),
                        jnp.maximum(occ[2 * a + 1, 2 * c], occ[2 * a + 1, 2 * c + 1]),
                    ).astype(F32)
                    outc[k, a, c, t, s128] = (value * m).astype(BF16)

            m2l_pass(
                sources,
                lambda s, c: (cs[s, c, 0, q, t, :], cs[s, c, 1, q, t, :]),
                lambda code: (tc[0, code, t, s128], tc[1, code, t, s128]),
                None if start else (lambda k, a, c: accc[k, a, c, q, t, :]),
                store, half,
            )

        loop(0, (nt2 // 8) * tiles2, tile)

    halves = [range(2 * h, 2 * h + 2) for h in range(rows // 2)]
    last = rows // 2 - 1
    fine(0, range(2, 6), True, False)
    hand_on(1)
    fine(last, range(0, 4), True, False)
    for copy in own_edges:
        copy.wait_recv()
    fill_edges(0, own_flag, rows, range(rows))
    local[6].wait()
    aggregate(rows // 2)
    hand_on(2)
    aggregate(rows // 2 + 1)
    coarse(range(2, 4), True, False)
    hand_on(3)

    have(cross_edges, 1, cross_flag, cross_row, halves[0])
    aggregate(cross_row // 2)
    flag_on.wait_recv()
    to_flags = pltpu.make_async_copy(flagv.at[1], flags.at[1], ls.at[7])
    to_flags.start()
    to_flags.wait()
    pass_edges(0)

    @pl.when(yh == 0)
    def _():
        fine(last, range(4, 6), False, True)

    @pl.when(yh == 1)
    def _():
        fine(0, range(0, 2), False, True)

    pass_edges(1)
    have(cross_edges, 1, cross_flag, cross_row, halves[1])
    aggregate(cross_row // 2 + 1)
    pass_edges(2)

    @pl.when(yh == 0)
    def _():
        coarse(range(4, 6), False, False)

    @pl.when(yh == 1)
    def _():
        coarse(range(0, 2), False, False)

    pass_edges(3)
    have(other_edges, 2, other_flag, other_row, halves[0])
    aggregate(other_row // 2)

    @pl.when(yh == 0)
    def _():
        fine(0, range(0, 2), False, True)
        coarse(range(0, 1), False, False)

    @pl.when(yh == 1)
    def _():
        fine(last, range(4, 6), False, True)
        coarse(range(4, 5), False, False)

    have(other_edges, 2, other_flag, other_row, halves[1])
    aggregate(other_row // 2 + 1)

    @pl.when(yh == 0)
    def _():
        coarse(range(1, 2), False, True)

    @pl.when(yh == 1)
    def _():
        coarse(range(5, 6), False, True)

    for copy in [flag_copy, flag_on] + first + own_edges + onward + cross_edges + other_edges:
        copy.wait_send()


def emit_kernel(fine, coarse, outf, outc, sems):
    copies = [pltpu.make_async_copy(fine, outf, sems.at[0]), pltpu.make_async_copy(coarse, outc, sems.at[1])]
    for copy in copies:
        copy.start()
    for copy in copies:
        copy.wait()


def local_step(nb, nd, pattern, occupied, trans_fine, trans_coarse, theta_weights, phi_matrix, child_phase):
    _, rows, cols, nt, nph = pattern.shape
    far, nt2, nph2 = trans_coarse.shape[1:]
    shape = jax.ShapeDtypeStruct
    tile2 = nph2 // 128
    fine, coarse = pl.pallas_call(
        functools.partial(kernel, nb, nd),
        out_shape=(
            shape((2, rows, cols, nt, nph), BF16),
            shape((2, rows // 2, cols // 2, nt2, nph2), BF16),
        ),
        in_specs=[HBM] * 7,
        out_specs=(VMEM, VMEM),
        scratch_shapes=[
            pltpu.VMEM((2, rows, cols, nt, nph), BF16),
            pltpu.VMEM((2, 2, rows, cols, nt, nph), BF16),
            pltpu.VMEM((3, rows, cols, 2, nph), BF16),
            pltpu.VMEM((3, rows, cols, 2, nph), BF16),
            pltpu.VMEM((3, 2, rows, cols, 2, nph), BF16),
            pltpu.VMEM((2, rows, cols), jnp.int32),
            pltpu.SMEM((2, rows, cols), jnp.int32),
            pltpu.SMEM((rows, cols), jnp.int32),
            pltpu.VMEM((2, far, nt, nph), BF16),
            pltpu.VMEM((2, far, nt2, nph2), BF16),
            pltpu.VMEM((4, nt2), BF16),
            pltpu.VMEM(phi_matrix.shape, BF16),
            pltpu.VMEM((4, nt2, nph2), F32),
            pltpu.VMEM((3 * rows, cols, 2, nt + 16, nph), F32),
            pltpu.VMEM((2, far, nt, nph), F32),
            pltpu.VMEM((2, far, nt2, nph2), F32),
            pltpu.VMEM((4, nt2, 128), F32),
            pltpu.VMEM((2 * (cols // 2) * 2 * nt2, nph), BF16),
            pltpu.VMEM((2 * (cols // 2) * 2 * nt2, nph2), F32),
            pltpu.VMEM((3 * rows // 2, cols // 2, 2, tile2, nt2, 128), F32),
            pltpu.VMEM((2, 4, tile2, nt2, 128), F32),
            pltpu.VMEM((2, rows, cols, nt, nph), F32),
            pltpu.VMEM((2, rows // 2, cols // 2, tile2, nt2, 128), F32),
            pltpu.SemaphoreType.DMA((32,)),
            pltpu.SemaphoreType.DMA((32,)),
            pltpu.SemaphoreType.DMA((8,)),
        ],
        compiler_params=pltpu.CompilerParams(
            collective_id=0, has_side_effects=True, vmem_limit_bytes=32 * 1024 * 1024
        ),
        name="main",
    )(
        *(
            pltpu.with_memory_space_constraint(x, pltpu.HBM)
            for x in (pattern, occupied, trans_fine, trans_coarse, theta_weights.T, phi_matrix, child_phase)
        )
    )
    return pl.pallas_call(
        emit_kernel,
        out_shape=(shape(fine.shape, BF16), shape(coarse.shape, BF16)),
        in_specs=[ANY] * 2,
        out_specs=(ANY,) * 2,
        scratch_shapes=[pltpu.SemaphoreType.DMA((2,))],
        compiler_params=pltpu.CompilerParams(vmem_limit_bytes=1024 * 1024),
        name="emit",
    )(fine, coarse)


def solution(mesh):
    return jax.shard_map(
        functools.partial(local_step, mesh.shape["box"], mesh.shape["dir"]),
        mesh=mesh,
        in_specs=(
            P(None, "box", None, "dir", None),
            P("box", None),
            P(None, None, "dir", None),
            P(None, None, "dir", None),
            P("dir", None),
            P(),
            P(None, "dir", None),
        ),
        out_specs=(P(None, "box", None, "dir", None), P(None, "box", None, "dir", None)),
        check_vma=False,
    )
```

```python
import functools

import jax
import jax.numpy as jnp
from jax import lax
from jax.experimental import pallas as pl
from jax.experimental.pallas import tpu as pltpu
from jax.sharding import PartitionSpec as P

MESH = pl.DeviceIdType.MESH
F32, BF16 = jnp.float32, jnp.bfloat16
VMEM = pl.BlockSpec(memory_space=pltpu.VMEM)
HBM = pl.BlockSpec(memory_space=pltpu.HBM)
ANY = pl.BlockSpec(memory_space=pl.ANY)

CODES = {
    pq: code
    for code, pq in enumerate(
        (p, q) for p in range(-3, 4) for q in range(-3, 4) if max(abs(p), abs(q)) >= 2
    )
}


def loop(start, stop, body):
    def step(i, carry):
        body(i)
        return carry

    lax.fori_loop(start, stop, step, 0)


def lanes(i):
    return pl.ds(pl.multiple_of(i * 128, 128), 128)


def m2l_pass(sources, load, table, first, store, ncols):
    def parent_sums(parent, window):
        acc = {}
        if first is not None:
            for a in range(2):
                for b in range(2):
                    acc[(a, b)] = tuple(first(k, a, 2 * parent + b) for k in range(2))
        for s in sources:
            group = {}
            for u in window:
                pairs = [
                    (a, b, CODES[(s - 2 - a, u - 2 - b)])
                    for a in range(2)
                    for b in range(2)
                    if (s - 2 - a, u - 2 - b) in CODES
                ]
                if not pairs:
                    continue
                sre, sim = load(s, 2 * parent + u - 2)
                for a, b, code in pairs:
                    tre, tim = table(code)
                    re = sre * tre - sim * tim
                    im = sre * tim + sim * tre
                    if (a, b) in group:
                        re, im = group[(a, b)][0] + re, group[(a, b)][1] + im
                    group[(a, b)] = (re, im)
            for place, value in group.items():
                value = tuple(v.astype(F32) for v in value)
                if place in acc:
                    value = (acc[place][0] + value[0], acc[place][1] + value[1])
                acc[place] = value
        for (a, b), value in acc.items():
            for k in range(2):
                store(k, a, 2 * parent + b, value[k])

    parent_sums(0, range(2, 6))
    loop(1, ncols // 2 - 1, lambda parent: parent_sums(parent, range(6)))
    parent_sums(ncols // 2 - 1, range(4))


def kernel(
    nb, nd, pat, occ_any, trf_any, trc_any, wts_any, phi_any, child_any,
    outf, outc,
    patv, nbr, lasts, thb, tha, flagv, flags, occ, trf, trc, wts, phi, child,
    xs, xp, tf, band, tp, full, cs, phase, accf, accc,
    ss, rs, ls,
):
    b, d = lax.axis_index("box"), lax.axis_index("dir")
    yh = lax.rem(b, 2)
    cross = {"box": b + 1 - 2 * yh}
    ahead = {"box": lax.rem(b + 2 - 4 * yh + nb, nb)}
    behind = {"box": lax.rem(b - 2 + 4 * yh + nb, nb)}
    up, down = {"dir": lax.rem(d + 1, nd)}, {"dir": lax.rem(d + nd - 1, nd)}
    rows, cols, nt, nph = patv.shape[1:]
    nt2, nph2 = trc.shape[2:]
    far = trf.shape[1]
    half = cols // 2
    tiles, tiles2 = nph // 128, nph2 // 128

    bar = pltpu.get_barrier_semaphore()
    beyond = {"box": lax.rem(b - 1 + 2 * yh + nb, nb)}
    for p in (cross, ahead, behind, up, down, beyond):
        pl.semaphore_signal(bar, inc=1, device_id=p, device_id_type=MESH)
    local = [
        pltpu.make_async_copy(src, dst, ls.at[i])
        for i, (src, dst) in enumerate(
            (
                (pat, patv), (occ_any, occ), (trf_any, trf), (trc_any, trc), (wts_any, wts),
                (child_any, child), (phi_any, phi),
            )
        )
    ]
    for copy in local:
        copy.start()

    count = iter(range(64))

    class Copy:
        def __init__(self, copy, sends, gets):
            self.copy, self.sends, self.gets = copy, sends, gets

        def start(self):
            self.under(self.sends, self.copy.start)

        def wait_recv(self):
            self.under(self.gets, self.copy.wait_recv)

        def wait_send(self):
            self.under(self.sends, self.copy.wait_send)

        def under(self, condition, action):
            if condition is None:
                action()
            else:
                pl.when(condition)(action)

    not_first, not_last = d > 0, d < nd - 1
    reach = b + 2 - 4 * yh
    from_b = b - 2 + 4 * yh
    has_o = (b - 1 + 2 * yh >= 0) & (b - 1 + 2 * yh < nb)
    onto = (reach >= 0) & (reach < nb)
    off = (from_b >= 0) & (from_b < nb)

    def send(src, dst, device):
        i = next(count)
        copy = pltpu.make_async_remote_copy(
            src_ref=src, dst_ref=dst, send_sem=ss.at[i], recv_sem=rs.at[i],
            device_id=device, device_id_type=MESH,
        )
        sends, gets = None, None
        if device is up:
            sends, gets = not_last, not_first
        elif device is down:
            sends, gets = not_first, not_last
        elif device is ahead:
            sends, gets = onto, off
        elif device is beyond:
            sends, gets = has_o, has_o
        copy = Copy(copy, sends, gets)
        copy.start()
        return copy

    has_up = (d < nd - 1).astype(F32)
    has_down = (d > 0).astype(F32)
    other = b - 1 + 2 * yh
    has_other = ((other >= 0).astype(jnp.int32) * (other < nb).astype(jnp.int32)).astype(F32)

    def fill(slot, read, flag, first_row, r, some):
        for c in some:
            m = flag(r, c)
            for k in range(2):
                value = read(k, r, c).astype(F32) * m
                xs[first_row + r, c, k] = value
                xp[first_row + r, c, k, 0:nt, :] = value.astype(BF16)
        for c in some:
            pair = [xs[first_row + r, c, k, nt - 1 : nt, :] for k in range(2)]
            lasts[slot, r, c] = jnp.concatenate(pair, axis=0).astype(BF16)

    def fill_edges(slot, flag, first_row, start, some):
        zeros = jnp.zeros((nt2 - nt - 3, nph), F32)

        def row(i):
            r = start + i
            for c in range(cols):
                m = flag(r, c) * has_up
                before = thb[slot, r, c].astype(F32) * has_down
                for k in range(2):
                    after = tha[slot, k, r, c].astype(F32) * m
                    around = jnp.concatenate([after, before[k : k + 1], zeros], axis=0)
                    xp[first_row + r, c, k, nt:nt2, :] = around.astype(BF16)

        loop(0, some, row)

    def own_flag(r, c):
        return occ[r, c].astype(F32)

    def cross_flag(r, c):
        return flags[0, r, c].astype(F32)

    def other_flag(r, c):
        return flags[1, r, c].astype(F32) * has_other

    def clear(ref, condition):
        @pl.when(condition)
        def _():
            def row(r):
                ref[:, r] = jnp.zeros(ref[:, r].shape, ref.dtype)

            loop(0, rows, row)

    no_other = (other < 0) | (other >= nb)
    clear(nbr.at[1], no_other)
    clear(thb, d == 0)
    for slot in range(3):
        clear(tha.at[slot], d == nd - 1)

    @pl.when(no_other)
    def _():
        flagv[1] = jnp.zeros((rows, cols), jnp.int32)

    local[0].wait()
    local[1].wait()
    loop(0, rows, lambda r: fill(0, lambda k, r, c: patv[k, r, c], own_flag, rows, r, range(cols)))

    pl.semaphore_wait(bar, 6)
    def sent_row(i):
        return lax.rem(i // 2 + 2 * (1 - yh), rows)

    def got_row(i):
        return lax.rem(i // 2 + 2 * yh, rows)

    def piece(ref, r, i):
        return ref.at[:, r, half * (i % 2) : half * (i % 2) + half]

    def send_piece(i):
        return send(piece(pat, sent_row(i), i), piece(nbr.at[0], sent_row(i), i), cross)

    first = [send_piece(0), send_piece(1)]
    flag_copy = send(occ_any, flagv.at[0], cross)
    own_edges = [
        send(lasts.at[0], thb.at[0], up),
        send(pat.at[:, :, :, 0:2, :], tha.at[0], down),
    ]
    onward, straight = [None] * (2 * rows), 2 * rows - 2
    for i in range(2, 2 * rows):
        first.append(send_piece(i))
        if i >= straight:
            onward[i] = send(piece(pat, sent_row(i), i), piece(nbr.at[1], sent_row(i), i), beyond)
    cross_edges, other_edges = [], []
    cross_row, other_row = 2 * rows * (1 - yh), 2 * rows * yh

    def columns(i):
        return range(half * (i % 2), half * (i % 2) + half)

    def hand_on(i):
        r = got_row(i)
        first[i].wait_recv()
        if i < straight:
            onward[i] = send(piece(nbr.at[0], r, i), piece(nbr.at[1], r, i), ahead)
        fill(1, lambda k, r, c: nbr[0, k, r, c], cross_flag, cross_row, r, columns(i))
        if i % 2:
            cross_edges.append(send(nbr.at[0, :, r, :, 0:2, :], tha.at[1, :, r], down))
            cross_edges.append(send(lasts.at[1, r], thb.at[1, r], up))

    def pass_edges(i):
        r = got_row(i)
        onward[i].wait_recv()
        fill(2, lambda k, r, c: nbr[1, k, r, c], other_flag, other_row, r, columns(i))
        if i % 2:
            other_edges.append(send(nbr.at[1, :, r, :, 0:2, :], tha.at[2, :, r], down))
            other_edges.append(send(lasts.at[2, r], thb.at[2, r], up))

    def have(edges, slot, flag, first_row, h):
        for copy in edges[4 * h : 4 * h + 4]:
            copy.wait_recv()
        fill_edges(slot, flag, first_row, got_row(4 * h), 2)

    local[2].wait()
    local[3].wait()

    def widen(i):
        for k in range(2):
            tf[k, i] = trf[k, i].astype(F32)

    loop(0, far, widen)
    eye = (
        lax.broadcasted_iota(jnp.int32, (nt2, nt2), 0) == lax.broadcasted_iota(jnp.int32, (nt2, nt2), 1)
    ).astype(F32)
    local[4].wait()
    w = wts[...].astype(F32)
    wide = band.shape[1]
    lane = lax.broadcasted_iota(jnp.int32, (nt2, wide), 1)
    place = jnp.bitwise_and(lane, nt2 - 1)
    source = jnp.where(place < nt + 2, place, jnp.where(place == nt + 2, -1, -8))
    step = source - jnp.right_shift(lax.broadcasted_iota(jnp.int32, (nt2, wide), 0), 1) + 1
    weights = jnp.zeros((nt2, wide), F32)
    for m in range(4):
        column = jnp.sum(eye * w[m : m + 1, :], axis=1, keepdims=True)
        weights = weights + jnp.where(step == m, jnp.broadcast_to(column, (nt2, wide)), 0.0)
    for g in range(wide // nt2):
        mine = (lane >= g * nt2) & (lane < (g + 1) * nt2)
        band[g * nt2 : (g + 1) * nt2, :] = jnp.where(mine, weights, 0.0).astype(BF16)
    local[5].wait()

    def phases(ab):
        angle = child[ab]
        phase[0, ab] = jnp.cos(angle)
        phase[1, ab] = jnp.sin(angle)

    loop(0, 4, phases)

    flag_copy.wait_recv()
    flag_on = send(flagv.at[0], flagv.at[1], ahead)
    to_flags = pltpu.make_async_copy(flagv.at[0], flags.at[0], ls.at[7])
    to_flags.start()
    to_flags.wait()
    def fine(block, sources, start, final, some):
        def tile(q):
            s128 = lanes(q)

            def store(k, a, c, value):
                r = 2 * block + a
                if not final:
                    accf[k, r, c, :, s128] = value
                else:
                    outf[k, r, c, :, s128] = (value * occ[r, c].astype(F32)).astype(BF16)

            m2l_pass(
                sources,
                lambda s, c: tuple(xs[rows - 2 + 2 * block + s, c, k, :, s128] for k in range(2)),
                lambda code: (tf[0, code, :, s128], tf[1, code, :, s128]),
                None if start else (lambda k, a, c: accf[k, 2 * block + a, c, :, s128]),
                store, cols,
            )

        loop(some[0], some[-1] + 1, tile)

    def aggregate(row):
        def part_of(part):
            for a in range(2):
                x = xp[2 * row + a, pl.ds(part * half, half)].reshape(half * 2 * nt2, nph)
                theta = jnp.dot(band[...], x, preferred_element_type=F32)
                tp[part, a * half * 2 * nt2 : (a + 1) * half * 2 * nt2, :] = theta.astype(BF16)
            full[part] = jnp.dot(tp[part], phi[...], preferred_element_type=F32)
            for q in range(tiles2):
                s = slice(128 * q, 128 * q + 128)
                ph = [(phase[0, ab, :, s], phase[1, ab, :, s]) for ab in range(4)]
                for parent in range(half // 2):
                    re = im = None
                    for a in range(2):
                        for bb in range(2):
                            at = (a * half + 2 * parent + bb) * 2 * nt2
                            fre = full[part, at : at + nt2, s]
                            fim = full[part, at + nt2 : at + 2 * nt2, s]
                            co, si = ph[2 * a + bb]
                            tre, tim = co * fre - si * fim, co * fim + si * fre
                            re, im = (tre, tim) if re is None else (re + tre, im + tim)
                    cs[row, part * (half // 2) + parent, 0, :, s] = re.astype(BF16)
                    cs[row, part * (half // 2) + parent, 1, :, s] = im.astype(BF16)

        for part in range(2):
            part_of(part)

    def coarse(sources, start, final, some=None):
        def tile(i):
            s128 = lanes(i)

            def store(k, a, c, value):
                if not final:
                    accc[k, a, c, :, s128] = value
                else:
                    m = jnp.maximum(
                        jnp.maximum(occ[2 * a, 2 * c], occ[2 * a, 2 * c + 1]),
                        jnp.maximum(occ[2 * a + 1, 2 * c], occ[2 * a + 1, 2 * c + 1]),
                    ).astype(F32)
                    outc[k, a, c, :, s128] = (value * m).astype(BF16)

            m2l_pass(
                sources,
                lambda s, c: (cs[s, c, 0, :, s128], cs[s, c, 1, :, s128]),
                lambda code: (trc[0, code, :, s128], trc[1, code, :, s128]),
                None if start else (lambda k, a, c: accc[k, a, c, :, s128]),
                store, half,
            )

        start_at, stop_at = (0, tiles2) if some is None else (some * tiles2 // 2, (some + 1) * tiles2 // 2)
        loop(start_at, stop_at, tile)

    last = rows // 2 - 1
    every = range(tiles)

    def by_side(when_0, when_1):
        pl.when(yh == 0)(when_0)
        pl.when(yh == 1)(when_1)

    def coarse_row(first_row, h):
        return first_row // 2 + lax.rem(h + yh, 2)

    fine(0, range(2, 6), True, False, [0])
    hand_on(0)
    fine(0, range(2, 6), True, False, [1])
    hand_on(1)
    fine(last, range(0, 4), True, False, [0])
    hand_on(2)
    fine(last, range(0, 4), True, False, [1])
    hand_on(3)
    by_side(
        lambda: fine(last, range(4, 6), False, True, every),
        lambda: fine(0, range(0, 2), False, True, every),
    )
    hand_on(4)
    for copy in own_edges:
        copy.wait_recv()
    fill_edges(0, own_flag, rows, 0, rows)
    local[6].wait()
    aggregate(rows // 2)
    hand_on(5)
    aggregate(rows // 2 + 1)
    hand_on(6)
    coarse(range(2, 4), True, False)
    hand_on(7)
    flag_on.wait_recv()
    to_flags = pltpu.make_async_copy(flagv.at[1], flags.at[1], ls.at[7])
    to_flags.start()
    to_flags.wait()
    for i in range(4):
        pass_edges(i)
    have(cross_edges, 1, cross_flag, cross_row, 0)
    aggregate(coarse_row(cross_row, 0))
    pass_edges(4)
    pass_edges(5)
    have(cross_edges, 1, cross_flag, cross_row, 1)
    aggregate(coarse_row(cross_row, 1))
    pass_edges(6)
    by_side(
        lambda: coarse(range(4, 6), False, False, 0),
        lambda: coarse(range(0, 2), False, False, 0),
    )
    pass_edges(7)
    by_side(
        lambda: coarse(range(4, 6), False, False, 1),
        lambda: coarse(range(0, 2), False, False, 1),
    )
    by_side(
        lambda: fine(0, range(0, 2), False, True, every),
        lambda: fine(last, range(4, 6), False, True, every),
    )
    have(other_edges, 2, other_flag, other_row, 0)
    aggregate(coarse_row(other_row, 0))

    def other_side(block, rows_of_block, coarse_source):
        coarse(range(coarse_source, coarse_source + 1), False, False)

    by_side(lambda: other_side(0, range(0, 2), 0), lambda: other_side(last, range(4, 6), 5))
    have(other_edges, 2, other_flag, other_row, 1)
    aggregate(coarse_row(other_row, 1))
    by_side(lambda: coarse(range(1, 2), False, True), lambda: coarse(range(4, 5), False, True))

    for copy in [flag_copy, flag_on] + first + own_edges + onward + cross_edges + other_edges:
        copy.wait_send()


def emit_kernel(fine, coarse, outf, outc, sems):
    copies = [pltpu.make_async_copy(fine, outf, sems.at[0]), pltpu.make_async_copy(coarse, outc, sems.at[1])]
    for copy in copies:
        copy.start()
    for copy in copies:
        copy.wait()


def local_step(nb, nd, pattern, occupied, trans_fine, trans_coarse, theta_weights, phi_matrix, child_phase):
    _, rows, cols, nt, nph = pattern.shape
    far, nt2, nph2 = trans_coarse.shape[1:]
    shape = jax.ShapeDtypeStruct
    fine, coarse = pl.pallas_call(
        functools.partial(kernel, nb, nd),
        out_shape=(
            shape((2, rows, cols, nt, nph), BF16),
            shape((2, rows // 2, cols // 2, nt2, nph2), BF16),
        ),
        in_specs=[HBM] * 7,
        out_specs=(VMEM, VMEM),
        scratch_shapes=[
            pltpu.VMEM((2, rows, cols, nt, nph), BF16),
            pltpu.VMEM((2, 2, rows, cols, nt, nph), BF16),
            pltpu.VMEM((3, rows, cols, 2, nph), BF16),
            pltpu.VMEM((3, rows, cols, 2, nph), BF16),
            pltpu.VMEM((3, 2, rows, cols, 2, nph), BF16),
            pltpu.VMEM((2, rows, cols), jnp.int32),
            pltpu.SMEM((2, rows, cols), jnp.int32),
            pltpu.SMEM((rows, cols), jnp.int32),
            pltpu.VMEM((2, far, nt, nph), BF16),
            pltpu.VMEM((2, far, nt2, nph2), BF16),
            pltpu.VMEM((4, nt2), BF16),
            pltpu.VMEM(phi_matrix.shape, BF16),
            pltpu.VMEM((4, nt2, nph2), F32),
            pltpu.VMEM((3 * rows, cols, 2, nt, nph), F32),
            pltpu.VMEM((3 * rows, cols, 2, nt2, nph), BF16),
            pltpu.VMEM((2, far, nt, nph), F32),
            pltpu.VMEM((cols * nt2, cols * nt2), BF16),
            pltpu.VMEM((2, 2 * (cols // 2) * 2 * nt2, nph), BF16),
            pltpu.VMEM((2, 2 * (cols // 2) * 2 * nt2, nph2), F32),
            pltpu.VMEM((3 * rows // 2, cols // 2, 2, nt2, nph2), BF16),
            pltpu.VMEM((2, 4, nt2, nph2), F32),
            pltpu.VMEM((2, rows, cols, nt, nph), F32),
            pltpu.VMEM((2, rows // 2, cols // 2, nt2, nph2), F32),
            pltpu.SemaphoreType.DMA((40,)),
            pltpu.SemaphoreType.DMA((40,)),
            pltpu.SemaphoreType.DMA((8,)),
        ],
        compiler_params=pltpu.CompilerParams(
            collective_id=0, has_side_effects=True, vmem_limit_bytes=32 * 1024 * 1024
        ),
        name="main",
    )(
        *(
            pltpu.with_memory_space_constraint(x, pltpu.HBM)
            for x in (pattern, occupied, trans_fine, trans_coarse, theta_weights.T, phi_matrix, child_phase)
        )
    )
    return pl.pallas_call(
        emit_kernel,
        out_shape=(shape(fine.shape, BF16), shape(coarse.shape, BF16)),
        in_specs=[ANY] * 2,
        out_specs=(ANY,) * 2,
        scratch_shapes=[pltpu.SemaphoreType.DMA((2,))],
        compiler_params=pltpu.CompilerParams(vmem_limit_bytes=1024 * 1024),
        name="emit",
    )(fine, coarse)


def solution(mesh):
    return jax.shard_map(
        functools.partial(local_step, mesh.shape["box"], mesh.shape["dir"]),
        mesh=mesh,
        in_specs=(
            P(None, "box", None, "dir", None),
            P("box", None),
            P(None, None, "dir", None),
            P(None, None, "dir", None),
            P("dir", None),
            P(),
            P(None, "dir", None),
        ),
        out_specs=(P(None, "box", None, "dir", None), P(None, "box", None, "dir", None)),
        check_vma=False,
    )
```

```python
import functools

import jax
import jax.numpy as jnp
from jax import lax
from jax.experimental import pallas as pl
from jax.experimental.pallas import tpu as pltpu
from jax.sharding import PartitionSpec as P

MESH = pl.DeviceIdType.MESH
F32, BF16 = jnp.float32, jnp.bfloat16
VMEM = pl.BlockSpec(memory_space=pltpu.VMEM)
HBM = pl.BlockSpec(memory_space=pltpu.HBM)
ANY = pl.BlockSpec(memory_space=pl.ANY)

CODES = {
    pq: code
    for code, pq in enumerate(
        (p, q) for p in range(-3, 4) for q in range(-3, 4) if max(abs(p), abs(q)) >= 2
    )
}


def loop(start, stop, body):
    def step(i, carry):
        body(i)
        return carry

    lax.fori_loop(start, stop, step, 0)


def lanes(i):
    return pl.ds(pl.multiple_of(i * 128, 128), 128)


def m2l_pass(sources, load, table, first, store, ncols):
    def parent_sums(parent, window):
        acc = {}
        if first is not None:
            for a in range(2):
                for b in range(2):
                    acc[(a, b)] = tuple(first(k, a, 2 * parent + b) for k in range(2))
        for s in sources:
            group = {}
            for u in window:
                pairs = [
                    (a, b, CODES[(s - 2 - a, u - 2 - b)])
                    for a in range(2)
                    for b in range(2)
                    if (s - 2 - a, u - 2 - b) in CODES
                ]
                if not pairs:
                    continue
                sre, sim = load(s, 2 * parent + u - 2)
                for a, b, code in pairs:
                    tre, tim = table(code)
                    re = sre * tre - sim * tim
                    im = sre * tim + sim * tre
                    if (a, b) in group:
                        re, im = group[(a, b)][0] + re, group[(a, b)][1] + im
                    group[(a, b)] = (re, im)
            for place, value in group.items():
                value = tuple(v.astype(F32) for v in value)
                if place in acc:
                    value = (acc[place][0] + value[0], acc[place][1] + value[1])
                acc[place] = value
        for (a, b), value in acc.items():
            for k in range(2):
                store(k, a, 2 * parent + b, value[k])

    parent_sums(0, range(2, 6))
    loop(1, ncols // 2 - 1, lambda parent: parent_sums(parent, range(6)))
    parent_sums(ncols // 2 - 1, range(4))


def kernel(
    nb, nd, pat, occ_any, trf_any, trc_any, wts_any, phi_any, child_any,
    outf, outc,
    patv, nbr, lasts, thb, tha, flagv, flags, occ, trf, trc, wts, phi, child,
    xs, xp, tf, band, tp, full, cs, phase, accf, accc,
    ss, rs, ls,
):
    b, d = lax.axis_index("box"), lax.axis_index("dir")
    yh = lax.rem(b, 2)
    cross = {"box": b + 1 - 2 * yh}
    ahead = {"box": lax.rem(b + 2 - 4 * yh + nb, nb)}
    behind = {"box": lax.rem(b - 2 + 4 * yh + nb, nb)}
    up, down = {"dir": lax.rem(d + 1, nd)}, {"dir": lax.rem(d + nd - 1, nd)}
    rows, cols, nt, nph = patv.shape[1:]
    nt2, nph2 = trc.shape[2:]
    far = trf.shape[1]
    half = cols // 2
    tiles, tiles2 = nph // 128, nph2 // 128

    bar = pltpu.get_barrier_semaphore()
    beyond = {"box": lax.rem(b - 1 + 2 * yh + nb, nb)}
    for p in (cross, ahead, behind, up, down, beyond):
        pl.semaphore_signal(bar, inc=1, device_id=p, device_id_type=MESH)
    local = [
        pltpu.make_async_copy(src, dst, ls.at[i])
        for i, (src, dst) in enumerate(
            (
                (pat, patv), (occ_any, occ), (trf_any, trf), (trc_any, trc), (wts_any, wts),
                (child_any, child), (phi_any, phi),
            )
        )
    ]
    for copy in local:
        copy.start()

    count = iter(range(64))

    class Copy:
        def __init__(self, copy, sends, gets):
            self.copy, self.sends, self.gets = copy, sends, gets

        def start(self):
            self.under(self.sends, self.copy.start)

        def wait_recv(self):
            self.under(self.gets, self.copy.wait_recv)

        def wait_send(self):
            self.under(self.sends, self.copy.wait_send)

        def under(self, condition, action):
            if condition is None:
                action()
            else:
                pl.when(condition)(action)

    not_first, not_last = d > 0, d < nd - 1
    reach = b + 2 - 4 * yh
    from_b = b - 2 + 4 * yh
    has_o = (b - 1 + 2 * yh >= 0) & (b - 1 + 2 * yh < nb)
    onto = (reach >= 0) & (reach < nb)
    off = (from_b >= 0) & (from_b < nb)

    def send(src, dst, device):
        i = next(count)
        copy = pltpu.make_async_remote_copy(
            src_ref=src, dst_ref=dst, send_sem=ss.at[i], recv_sem=rs.at[i],
            device_id=device, device_id_type=MESH,
        )
        sends, gets = None, None
        if device is up:
            sends, gets = not_last, not_first
        elif device is down:
            sends, gets = not_first, not_last
        elif device is ahead:
            sends, gets = onto, off
        elif device is beyond:
            sends, gets = has_o, has_o
        copy = Copy(copy, sends, gets)
        copy.start()
        return copy

    has_up = (d < nd - 1).astype(F32)
    has_down = (d > 0).astype(F32)
    other = b - 1 + 2 * yh
    has_other = ((other >= 0).astype(jnp.int32) * (other < nb).astype(jnp.int32)).astype(F32)

    def fill(slot, read, flag, first_row, r, some):
        for c in some:
            m = flag(r, c)
            for k in range(2):
                value = read(k, r, c).astype(F32) * m
                xs[first_row + r, c, k] = value
                xp[first_row + r, c, k, 0:nt, :] = value.astype(BF16)
        for c in some:
            pair = [xs[first_row + r, c, k, nt - 1 : nt, :] for k in range(2)]
            lasts[slot, r, c] = jnp.concatenate(pair, axis=0).astype(BF16)

    def fill_edges(slot, flag, first_row, start, some):
        zeros = jnp.zeros((nt2 - nt - 3, nph), F32)

        def row(i):
            r = start + i
            for c in range(cols):
                m = flag(r, c) * has_up
                before = thb[slot, r, c].astype(F32) * has_down
                for k in range(2):
                    after = tha[slot, k, r, c].astype(F32) * m
                    around = jnp.concatenate([after, before[k : k + 1], zeros], axis=0)
                    xp[first_row + r, c, k, nt:nt2, :] = around.astype(BF16)

        loop(0, some, row)

    def own_flag(r, c):
        return occ[r, c].astype(F32)

    def cross_flag(r, c):
        return flags[0, r, c].astype(F32)

    def other_flag(r, c):
        return flags[1, r, c].astype(F32) * has_other

    def clear(ref, condition):
        @pl.when(condition)
        def _():
            def row(r):
                ref[:, r] = jnp.zeros(ref[:, r].shape, ref.dtype)

            loop(0, rows, row)

    no_other = (other < 0) | (other >= nb)
    clear(nbr.at[1], no_other)
    clear(thb, d == 0)
    for slot in range(3):
        clear(tha.at[slot], d == nd - 1)

    @pl.when(no_other)
    def _():
        flagv[1] = jnp.zeros((rows, cols), jnp.int32)

    local[0].wait()
    local[1].wait()
    loop(0, rows, lambda r: fill(0, lambda k, r, c: patv[k, r, c], own_flag, rows, r, range(cols)))

    pl.semaphore_wait(bar, 6)
    def sent_row(i):
        return lax.rem(i // 2 + 2 * (1 - yh), rows)

    def got_row(i):
        return lax.rem(i // 2 + 2 * yh, rows)

    def piece(ref, r, i):
        return ref.at[:, r, half * (i % 2) : half * (i % 2) + half]

    def send_piece(i):
        return send(piece(pat, sent_row(i), i), piece(nbr.at[0], sent_row(i), i), cross)

    first = [send_piece(0), send_piece(1)]
    flag_copy = send(occ_any, flagv.at[0], cross)
    own_edges = [
        send(lasts.at[0], thb.at[0], up),
        send(pat.at[:, :, :, 0:2, :], tha.at[0], down),
    ]
    onward, straight = [None] * (2 * rows), 2 * rows - 2
    for i in range(2, 2 * rows):
        first.append(send_piece(i))
        if i >= straight:
            onward[i] = send(piece(pat, sent_row(i), i), piece(nbr.at[1], sent_row(i), i), beyond)
    cross_edges, other_edges = [], []
    cross_row, other_row = 2 * rows * (1 - yh), 2 * rows * yh

    def columns(i):
        return range(half * (i % 2), half * (i % 2) + half)

    def hand_on(i):
        r = got_row(i)
        first[i].wait_recv()
        if i < straight:
            onward[i] = send(piece(nbr.at[0], r, i), piece(nbr.at[1], r, i), ahead)
        fill(1, lambda k, r, c: nbr[0, k, r, c], cross_flag, cross_row, r, columns(i))
        if i % 2:
            cross_edges.append(send(nbr.at[0, :, r, :, 0:2, :], tha.at[1, :, r], down))
            cross_edges.append(send(lasts.at[1, r], thb.at[1, r], up))

    def pass_edges(i):
        r = got_row(i)
        onward[i].wait_recv()
        fill(2, lambda k, r, c: nbr[1, k, r, c], other_flag, other_row, r, columns(i))
        if i % 2:
            other_edges.append(send(nbr.at[1, :, r, :, 0:2, :], tha.at[2, :, r], down))
            other_edges.append(send(lasts.at[2, r], thb.at[2, r], up))

    def have(edges, slot, flag, first_row, h):
        for copy in edges[4 * h : 4 * h + 4]:
            copy.wait_recv()
        fill_edges(slot, flag, first_row, got_row(4 * h), 2)

    local[2].wait()
    local[3].wait()

    def widen(i):
        for k in range(2):
            tf[k, i] = trf[k, i].astype(F32)

    loop(0, far, widen)
    eye = (
        lax.broadcasted_iota(jnp.int32, (nt2, nt2), 0) == lax.broadcasted_iota(jnp.int32, (nt2, nt2), 1)
    ).astype(F32)
    local[4].wait()
    w = wts[...].astype(F32)
    wide = band.shape[1]
    lane = lax.broadcasted_iota(jnp.int32, (nt2, wide), 1)
    place = jnp.bitwise_and(lane, nt2 - 1)
    source = jnp.where(place < nt + 2, place, jnp.where(place == nt + 2, -1, -8))
    step = source - jnp.right_shift(lax.broadcasted_iota(jnp.int32, (nt2, wide), 0), 1) + 1
    weights = jnp.zeros((nt2, wide), F32)
    for m in range(4):
        column = jnp.sum(eye * w[m : m + 1, :], axis=1, keepdims=True)
        weights = weights + jnp.where(step == m, jnp.broadcast_to(column, (nt2, wide)), 0.0)
    for g in range(wide // nt2):
        mine = (lane >= g * nt2) & (lane < (g + 1) * nt2)
        band[g * nt2 : (g + 1) * nt2, :] = jnp.where(mine, weights, 0.0).astype(BF16)
    local[5].wait()

    def phases(ab):
        angle = child[ab]
        phase[0, ab] = jnp.cos(angle)
        phase[1, ab] = jnp.sin(angle)

    loop(0, 4, phases)

    flag_copy.wait_recv()
    flag_on = send(flagv.at[0], flagv.at[1], ahead)
    to_flags = pltpu.make_async_copy(flagv.at[0], flags.at[0], ls.at[7])
    to_flags.start()
    to_flags.wait()
    def fine(block, sources, start, final, some):
        def tile(q):
            s128 = lanes(q)

            def store(k, a, c, value):
                r = 2 * block + a
                if not final:
                    accf[k, r, c, :, s128] = value
                else:
                    outf[k, r, c, :, s128] = (value * occ[r, c].astype(F32)).astype(BF16)

            m2l_pass(
                sources,
                lambda s, c: tuple(xs[rows - 2 + 2 * block + s, c, k, :, s128] for k in range(2)),
                lambda code: (tf[0, code, :, s128], tf[1, code, :, s128]),
                None if start else (lambda k, a, c: accf[k, 2 * block + a, c, :, s128]),
                store, cols,
            )

        loop(some[0], some[-1] + 1, tile)

    def aggregate(row):
        def part_of(part):
            for a in range(2):
                x = xp[2 * row + a, pl.ds(part * half, half)].reshape(half * 2 * nt2, nph)
                theta = jnp.dot(band[...], x, preferred_element_type=F32)
                tp[part, a * half * 2 * nt2 : (a + 1) * half * 2 * nt2, :] = theta.astype(BF16)
            full[part] = jnp.dot(tp[part], phi[...], preferred_element_type=F32)
            for q in range(tiles2):
                s = slice(128 * q, 128 * q + 128)
                ph = [(phase[0, ab, :, s], phase[1, ab, :, s]) for ab in range(4)]
                for parent in range(half // 2):
                    re = im = None
                    for a in range(2):
                        for bb in range(2):
                            at = (a * half + 2 * parent + bb) * 2 * nt2
                            fre = full[part, at : at + nt2, s]
                            fim = full[part, at + nt2 : at + 2 * nt2, s]
                            co, si = ph[2 * a + bb]
                            tre, tim = co * fre - si * fim, co * fim + si * fre
                            re, im = (tre, tim) if re is None else (re + tre, im + tim)
                    cs[row, part * (half // 2) + parent, 0, :, s] = re.astype(BF16)
                    cs[row, part * (half // 2) + parent, 1, :, s] = im.astype(BF16)

        for part in range(2):
            part_of(part)

    def coarse(sources, start, final, some=None):
        def tile(i):
            s128 = lanes(i)

            def store(k, a, c, value):
                if not final:
                    accc[k, a, c, :, s128] = value
                else:
                    m = jnp.maximum(
                        jnp.maximum(occ[2 * a, 2 * c], occ[2 * a, 2 * c + 1]),
                        jnp.maximum(occ[2 * a + 1, 2 * c], occ[2 * a + 1, 2 * c + 1]),
                    ).astype(F32)
                    outc[k, a, c, :, s128] = (value * m).astype(BF16)

            m2l_pass(
                sources,
                lambda s, c: (cs[s, c, 0, :, s128], cs[s, c, 1, :, s128]),
                lambda code: (trc[0, code, :, s128], trc[1, code, :, s128]),
                None if start else (lambda k, a, c: accc[k, a, c, :, s128]),
                store, half,
            )

        start_at, stop_at = (0, tiles2) if some is None else (some * tiles2 // 2, (some + 1) * tiles2 // 2)
        loop(start_at, stop_at, tile)

    last = rows // 2 - 1
    every = range(tiles)

    def by_side(when_0, when_1):
        pl.when(yh == 0)(when_0)
        pl.when(yh == 1)(when_1)

    def coarse_row(first_row, h):
        return first_row // 2 + lax.rem(h + yh, 2)

    fine(0, range(2, 6), True, False, [0])
    hand_on(0)
    fine(0, range(2, 6), True, False, [1])
    hand_on(1)
    fine(last, range(0, 4), True, False, [0])
    hand_on(2)
    fine(last, range(0, 4), True, False, [1])
    hand_on(3)
    by_side(
        lambda: fine(last, range(4, 6), False, True, every),
        lambda: fine(0, range(0, 2), False, True, every),
    )
    hand_on(4)
    for copy in own_edges:
        copy.wait_recv()
    fill_edges(0, own_flag, rows, 0, rows)
    local[6].wait()
    aggregate(rows // 2)
    hand_on(5)
    aggregate(rows // 2 + 1)
    hand_on(6)
    coarse(range(2, 4), True, False)
    hand_on(7)
    flag_on.wait_recv()
    to_flags = pltpu.make_async_copy(flagv.at[1], flags.at[1], ls.at[7])
    to_flags.start()
    to_flags.wait()
    for i in range(4):
        pass_edges(i)
    have(cross_edges, 1, cross_flag, cross_row, 0)
    aggregate(coarse_row(cross_row, 0))
    pass_edges(4)
    pass_edges(5)
    have(cross_edges, 1, cross_flag, cross_row, 1)
    aggregate(coarse_row(cross_row, 1))
    pass_edges(6)
    by_side(
        lambda: coarse(range(4, 6), False, False, 0),
        lambda: coarse(range(0, 2), False, False, 0),
    )
    pass_edges(7)
    by_side(
        lambda: coarse(range(4, 6), False, False, 1),
        lambda: coarse(range(0, 2), False, False, 1),
    )
    by_side(
        lambda: fine(0, range(0, 2), False, True, every),
        lambda: fine(last, range(4, 6), False, True, every),
    )
    have(other_edges, 2, other_flag, other_row, 0)
    aggregate(coarse_row(other_row, 0))

    def other_side(block, rows_of_block, coarse_source):
        coarse(range(coarse_source, coarse_source + 1), False, False)

    by_side(lambda: other_side(0, range(0, 2), 0), lambda: other_side(last, range(4, 6), 5))
    have(other_edges, 2, other_flag, other_row, 1)
    aggregate(coarse_row(other_row, 1))
    by_side(lambda: coarse(range(1, 2), False, True), lambda: coarse(range(4, 5), False, True))

    for copy in [flag_copy, flag_on] + first + own_edges + onward + cross_edges + other_edges:
        copy.wait_send()


def emit_kernel(fine, coarse, outf, outc, sems):
    pieces = [
        (src.at[k, r], dst.at[k, r])
        for src, dst in ((coarse, outc), (fine, outf))
        for k in range(src.shape[0])
        for r in range(src.shape[1])
    ]
    copies = [pltpu.make_async_copy(src, dst, sems.at[i]) for i, (src, dst) in enumerate(pieces)]
    for copy in copies:
        copy.start()
    for copy in copies:
        copy.wait()


def local_step(nb, nd, pattern, occupied, trans_fine, trans_coarse, theta_weights, phi_matrix, child_phase):
    _, rows, cols, nt, nph = pattern.shape
    far, nt2, nph2 = trans_coarse.shape[1:]
    shape = jax.ShapeDtypeStruct
    fine, coarse = pl.pallas_call(
        functools.partial(kernel, nb, nd),
        out_shape=(
            shape((2, rows, cols, nt, nph), BF16),
            shape((2, rows // 2, cols // 2, nt2, nph2), BF16),
        ),
        in_specs=[HBM] * 7,
        out_specs=(VMEM, VMEM),
        scratch_shapes=[
            pltpu.VMEM((2, rows, cols, nt, nph), BF16),
            pltpu.VMEM((2, 2, rows, cols, nt, nph), BF16),
            pltpu.VMEM((3, rows, cols, 2, nph), BF16),
            pltpu.VMEM((3, rows, cols, 2, nph), BF16),
            pltpu.VMEM((3, 2, rows, cols, 2, nph), BF16),
            pltpu.VMEM((2, rows, cols), jnp.int32),
            pltpu.SMEM((2, rows, cols), jnp.int32),
            pltpu.SMEM((rows, cols), jnp.int32),
            pltpu.VMEM((2, far, nt, nph), BF16),
            pltpu.VMEM((2, far, nt2, nph2), BF16),
            pltpu.VMEM((4, nt2), BF16),
            pltpu.VMEM(phi_matrix.shape, BF16),
            pltpu.VMEM((4, nt2, nph2), F32),
            pltpu.VMEM((3 * rows, cols, 2, nt, nph), F32),
            pltpu.VMEM((3 * rows, cols, 2, nt2, nph), BF16),
            pltpu.VMEM((2, far, nt, nph), F32),
            pltpu.VMEM((cols * nt2, cols * nt2), BF16),
            pltpu.VMEM((2, 2 * (cols // 2) * 2 * nt2, nph), BF16),
            pltpu.VMEM((2, 2 * (cols // 2) * 2 * nt2, nph2), F32),
            pltpu.VMEM((3 * rows // 2, cols // 2, 2, nt2, nph2), BF16),
            pltpu.VMEM((2, 4, nt2, nph2), F32),
            pltpu.VMEM((2, rows, cols, nt, nph), F32),
            pltpu.VMEM((2, rows // 2, cols // 2, nt2, nph2), F32),
            pltpu.SemaphoreType.DMA((40,)),
            pltpu.SemaphoreType.DMA((40,)),
            pltpu.SemaphoreType.DMA((8,)),
        ],
        compiler_params=pltpu.CompilerParams(
            collective_id=0, has_side_effects=True, vmem_limit_bytes=32 * 1024 * 1024
        ),
        name="main",
    )(
        *(
            pltpu.with_memory_space_constraint(x, pltpu.HBM)
            for x in (pattern, occupied, trans_fine, trans_coarse, theta_weights.T, phi_matrix, child_phase)
        )
    )
    return pl.pallas_call(
        emit_kernel,
        out_shape=(shape(fine.shape, BF16), shape(coarse.shape, BF16)),
        in_specs=[ANY] * 2,
        out_specs=(ANY,) * 2,
        scratch_shapes=[pltpu.SemaphoreType.DMA((2 * (rows + rows // 2),))],
        compiler_params=pltpu.CompilerParams(vmem_limit_bytes=1024 * 1024),
        name="emit",
    )(fine, coarse)


def solution(mesh):
    return jax.shard_map(
        functools.partial(local_step, mesh.shape["box"], mesh.shape["dir"]),
        mesh=mesh,
        in_specs=(
            P(None, "box", None, "dir", None),
            P("box", None),
            P(None, None, "dir", None),
            P(None, None, "dir", None),
            P("dir", None),
            P(),
            P(None, "dir", None),
        ),
        out_specs=(P(None, "box", None, "dir", None), P(None, "box", None, "dir", None)),
        check_vma=False,
    )
```
